32 devices in a mesh: shard: 8 (over z, x), tensor: 4 (over y, core).
Axes of the slice: x: 2, y: 2, z: 4, core: 2. Of those that a mesh axis runs over, the one named last changes fastest.
Arguments:
- mixer_gradient: float32 [3, 1536, 6144], P(None, 'shard', 'tensor'), may hold values from -60 to 60
- output_gradient: float32 [3, 1536, 3072], P(None, 'shard', 'tensor'), may hold values from -60 to 60
- mixer_basis: float32 [3, 1536, 256], P(None, 'shard'), may hold values from -0.21875 to 0.21875
- output_basis: float32 [3, 1536, 256], P(None, 'shard'), may hold values from -0.21875 to 0.21875
- mixer_mean: float32 [256, 3, 6144], P('shard', None, 'tensor'), may hold values from -4 to 4
- mixer_square: float32 [256, 3, 6144], P('shard', None, 'tensor'), may hold values from 0.05 to 2
- output_mean: float32 [256, 3, 3072], P('shard', None, 'tensor'), may hold values from -4 to 4
- output_square: float32 [256, 3, 3072], P('shard', None, 'tensor'), may hold values from 0.05 to 2
Outputs:
- mixer_update: float32 [3, 1536, 6144], P(None, 'shard', 'tensor')
- output_update: float32 [3, 1536, 3072], P(None, 'shard', 'tensor')
- mixer_moment: float32 [256, 3, 6144], P('shard', None, 'tensor')
- mixer_variance: float32 [256, 3, 6144], P('shard', None, 'tensor')
- output_moment: float32 [256, 3, 3072], P('shard', None, 'tensor')
- output_variance: float32 [256, 3, 3072], P('shard', None, 'tensor')
- mixer_refreshed: float32 [3, 1536, 256], P(None, 'shard')
- output_refreshed: float32 [3, 1536, 256], P(None, 'shard')
The draws below stay inside these ranges and needn't reach their ends.
All inputs are finite; a program needn't handle non-finite values.
Results may differ from the reference program's by a relative error of at most 0.0003.
Values sent between devices are 32-bit elements; how exact they have to be, the bound alone decides.
A program may use at most 128 MiB of HBM per device.

```python
import math
import jax
import jax.numpy as jnp
from jax import lax

D = 1536
INNER = 3072
MIXER = 6144
RANK = 256
LAYERS = 3
SWEEPS = 3
ADAM_STEP = 10


def rough_gradient(key, columns):
    key_noise, key_rows, key_cols = jax.random.split(key, 3)
    position = jnp.arange(D, dtype=jnp.float32) / D
    row_scale = jnp.exp(position[None, :, None] * math.log(3.0) + jax.random.uniform(key_rows, (LAYERS, D, 1), jnp.float32, 0.0, math.log(3.3)))
    col_scale = jnp.exp(jax.random.uniform(key_cols, (LAYERS, 1, columns), jnp.float32, 0.0, math.log(10.0)))
    noise = jax.random.normal(key_noise, (LAYERS, D, columns), jnp.float32)
    noise = jnp.clip(noise, -6.0, 6.0)
    return noise * row_scale * col_scale * 0.1


def draw_mixer_gradient(key, part):
    return rough_gradient(jax.random.fold_in(key, 11), MIXER)


def draw_output_gradient(key, part):
    return rough_gradient(jax.random.fold_in(key, 23), INNER)


def spiked(values, own_key, source, target, blocks, factor):
    owner, partner = [(jnp.arange(values.shape[axis_at]) // (values.shape[axis_at] // blocks)).reshape([-1 if axis == axis_at else 1 for axis in range(values.ndim)]) for axis_at in (source, target)]
    chosen = jax.random.permutation(own_key, blocks)[partner]
    strong = (owner == chosen) | (owner == (partner + blocks // 2) % blocks)
    return jnp.where(strong, factor * values, values)


def block_levels(key, extent, cuts, smallest, largest):
    def one(dim, parts):
        steps = jax.random.uniform(jax.random.fold_in(jax.random.fold_in(key, 6), dim), (parts,), jnp.float32, smallest / len(cuts), largest / len(cuts))
        return jnp.repeat(jnp.exp(steps), extent[dim] // parts).reshape((-1,) + (1,) * (len(extent) - dim - 1))

    gain = one(*cuts[0])
    for cut in cuts[1:]:
        gain = gain * one(*cut)
    return gain


def centred(rng, extent, deviation, bound, cuts=(), kind=jnp.bfloat16):
    factor_of = block_levels(rng, extent, cuts, -0.22, 0.18) if cuts else 1.0
    array = jax.random.normal(rng, extent, jnp.float32) * deviation * factor_of
    return jnp.minimum(jnp.maximum(array, -bound), bound).astype(kind)


def heavy_noise(own_key, dims, width, reach, cuts, heavy, kind=jnp.bfloat16):
    result = width * jax.random.normal(own_key, dims, jnp.float32)
    if cuts:
        result = result * block_levels(own_key, dims, cuts, -0.22, 0.18)
    return jnp.clip(spiked(result, jax.random.fold_in(own_key, 3), *heavy), -reach, reach).astype(kind)


def setup_inputs(seed: int = 0) -> dict:
    key_list = jax.random.split(jax.random.key(seed), 9)
    return {
        "mixer_gradient": draw_mixer_gradient(jax.random.fold_in(key_list[8], 71), 0),
        "output_gradient": draw_output_gradient(jax.random.fold_in(key_list[8], 71), 0),
        "mixer_basis": heavy_noise(key_list[2], (LAYERS, D, RANK), D ** -0.5, 0.21875, ((1, 8),), (1, 2, 8, 2.0), jnp.float32),
        "output_basis": heavy_noise(key_list[3], (LAYERS, D, RANK), D ** -0.5, 0.21875, ((1, 8),), (1, 2, 8, 2.0), jnp.float32),
        "mixer_mean": centred(key_list[4], (RANK, LAYERS, MIXER), 0.3, 4.0, ((0, 8), (2, 4)), jnp.float32),
        "mixer_square": jnp.clip(jnp.exp(math.log(2.0) - 3.6888794 * jax.random.uniform(key_list[5], (RANK, LAYERS, MIXER), jnp.float32) ** block_levels(key_list[5], (RANK, LAYERS, MIXER), ((0, 8), (2, 4)), -0.2, 0.2)), 0.05, 2.0),
        "output_mean": centred(key_list[6], (RANK, LAYERS, INNER), 0.3, 4.0, ((0, 8), (2, 4)), jnp.float32),
        "output_square": jnp.clip(jnp.exp(math.log(2.0) - 3.6888794 * jax.random.uniform(key_list[7], (RANK, LAYERS, INNER), jnp.float32) ** block_levels(key_list[7], (RANK, LAYERS, INNER), ((0, 8), (2, 4)), -0.2, 0.2)), 0.05, 2.0),
    }


highest = lax.Precision.HIGHEST
coeff_linear = 3.4445
coeff_square = -4.775
coeff_fourth = 2.0315
scale_epsilon = 1e-06
adam_epsilon = 1e-08
beta_first = 0.9
beta_second = 0.99

def adapt_matrix(gradient, basis, mean, square):
    projected = jnp.einsum('ldr,ldn->rln', basis, gradient, precision=highest)
    moment = beta_first * mean + (1.0 - beta_first) * projected
    variance = beta_second * square + (1.0 - beta_second) * projected * projected
    corrected = moment / (1.0 - beta_first ** ADAM_STEP)
    spread = jnp.sqrt(variance / (1.0 - beta_second ** ADAM_STEP)) + adam_epsilon
    direction = corrected / spread
    update = jnp.einsum('ldr,rln->ldn', basis, direction, precision=highest)
    power = jnp.einsum('ldn,rln->ldr', gradient, projected, precision=highest)
    return (update, moment, variance, power)

def orthogonalize(power):
    total = lax.optimization_barrier(jnp.sum(power * power, axis=(1, 2)))
    scale = jnp.sqrt(total) + scale_epsilon
    current = power / scale[:, None, None]
    for iteration in range(SWEEPS):
        gram = jnp.einsum('ldr,lds->lrs', current, current, precision=highest)
        squared = jnp.einsum('lrs,lst->lrt', gram, gram, precision=highest)
        polynomial = coeff_square * gram + coeff_fourth * squared
        current = coeff_linear * current + jnp.einsum('ldr,lrs->lds', current, polynomial, precision=highest)
    return current

def reference(mixer_gradient, output_gradient, mixer_basis, output_basis, mixer_mean, mixer_square, output_mean, output_square):
    mixer_update, mixer_moment, mixer_variance, mixer_power = adapt_matrix(mixer_gradient, mixer_basis, mixer_mean, mixer_square)
    output_update, output_moment, output_variance, output_power = adapt_matrix(output_gradient, output_basis, output_mean, output_square)
    mixer_refreshed = orthogonalize(mixer_power)
    output_refreshed = orthogonalize(output_power)
    return (mixer_update, output_update, mixer_moment, mixer_variance, output_moment, output_variance, mixer_refreshed, output_refreshed)
```

```python
import functools

import jax
import jax.numpy as jnp
from jax import lax
from jax.experimental import pallas as pl
from jax.experimental.pallas import tpu as pltpu
from jax.sharding import PartitionSpec as P

SWEEPS = 3
ADAM_STEP = 10

high = lax.Precision.HIGH
highest = lax.Precision.HIGHEST
coeff_linear = 3.4445
coeff_square = -4.775
coeff_fourth = 2.0315
scale_epsilon = 1e-06
adam_epsilon = 1e-08
beta_first = 0.9
beta_second = 0.99

MESH = pl.DeviceIdType.MESH
VMEM_LIMIT = 56 * 2**20


def adam_direction(mean, square, projected):
    moment = beta_first * mean + (1.0 - beta_first) * projected
    variance = beta_second * square + (1.0 - beta_second) * projected * projected
    corrected = moment / (1.0 - beta_first**ADAM_STEP)
    spread = jnp.sqrt(variance / (1.0 - beta_second**ADAM_STEP)) + adam_epsilon
    return (moment, variance, corrected / spread)


def remote(src, dst, send, recv, device):
    return pltpu.make_async_remote_copy(
        src_ref=src,
        dst_ref=dst,
        send_sem=send,
        recv_sem=recv,
        device_id=device,
        device_id_type=MESH,
    )


def place(groups):
    me = lax.axis_index("shard")
    return me // 2, lax.rem(me, 2)


def peer(line, side, step, groups):
    other = lax.rem(line + step, groups)
    return other, {"shard": other * 2 + side}


def greet(groups, tensor_peers=()):
    line, side = place(groups)
    barrier = pltpu.get_barrier_semaphore()
    devices = [peer(line, side, step, groups)[1] for step in range(1, groups)]
    devices.append({"shard": line * 2 + 1 - side})
    devices.extend({"tensor": other} for other in tensor_peers)
    for device in devices:
        pl.semaphore_signal(barrier, inc=1, device_id=device, device_id_type=MESH)
    pl.semaphore_wait(barrier, len(devices))


def units_of(refs):
    return [(which, layer) for layer in range(refs[0].shape[0]) for which in range(len(refs))]


def gather_one(groups, u, m, l, own, full, sems):
    line, side = place(groups)
    zs, zr, xs, xr = sems
    copies = []
    for step in range(1, groups):
        _, device = peer(line, side, step, groups)
        copy = remote(
            own[m].at[l], full[m].at[l, line, side], zs.at[u, step], zr.at[u, step], device
        )
        copy.start()
        copies.append(copy)
    pair = remote(
        own[m].at[l],
        full[m].at[l, line, side],
        xs.at[u, 0],
        xr.at[u, 0],
        {"shard": line * 2 + 1 - side},
    )
    pair.start()
    full[m][l, line, side] = own[m][l]
    return copies + [pair]


def gather_forward(groups, u, m, l, full, sems):
    line, side = place(groups)
    zs, zr, xs, xr = sems
    forwards = []
    for step in range(1, groups):
        source = lax.rem(line + groups - step, groups)
        block = full[m].at[l, source, side]
        landed = remote(
            block, block, zs.at[u, step], zr.at[u, step], {"shard": line * 2 + 1 - side}
        )
        landed.wait_recv()
        forward = remote(
            block, block, xs.at[u, step], xr.at[u, step], {"shard": line * 2 + 1 - side}
        )
        forward.start()
        forwards.append(forward)
    return forwards


def gather_finish(groups, u, m, l, full, sems, sent, forwards):
    line, side = place(groups)
    zs, zr, xs, xr = sems
    for copy in sent:
        copy.wait_send()
    for copy in forwards:
        copy.wait_send()
    for step in range(groups):
        source = lax.rem(line + groups - step, groups)
        block = full[m].at[l, source, 1 - side]
        remote(
            block, block, xs.at[u, step], xr.at[u, step], {"shard": line * 2 + 1 - side}
        ).wait_recv()


def scatter_pair(u, m, l, parts, pair_buf, sems, groups):
    line, side = place(groups)
    copy = remote(
        parts[m].at[l, :, 1 - side],
        pair_buf[m].at[l],
        sems[0].at[u],
        sems[1].at[u],
        {"shard": line * 2 + 1 - side},
    )
    copy.start()
    return copy


def scatter_line(u, m, l, parts, pair_buf, line_buf, copy, sems, groups):
    line, side = place(groups)
    copy.wait_recv()
    for g in range(groups):
        pair_buf[m][l, g] = pair_buf[m][l, g] + parts[m][l, g, side]
    sent = []
    for step in range(1, groups):
        other, device = peer(line, side, step, groups)
        out = remote(
            pair_buf[m].at[l, other],
            line_buf[m].at[l, step - 1],
            sems[2].at[u, step],
            sems[3].at[u, step],
            device,
        )
        out.start()
        sent.append(out)
    return sent


def scatter_sum(m, l, pair_buf, line_buf, sent, groups):
    line, _ = place(groups)
    total = pair_buf[m][l, line]
    for step in range(1, groups):
        sent[step - 1].wait_recv()
        total = total + line_buf[m][l, step - 1]
    return total


def reduce_kernel(groups, count, adam, *refs):
    parts = refs[:count]
    refs = refs[count:]
    if adam:
        means, squares = refs[:count], refs[count : 2 * count]
        refs = refs[2 * count :]
    full = refs[:count]
    refs = refs[count:]
    if adam:
        moments, variances, directions = (
            refs[:count],
            refs[count : 2 * count],
            refs[2 * count : 3 * count],
        )
        refs = refs[3 * count :]
    own, pair_buf, line_buf = (
        refs[:count],
        refs[count : 2 * count],
        refs[2 * count : 3 * count],
    )
    sems = refs[3 * count :]
    scatter_sems, gather_sems = sems[:4], sems[4:]
    greet(groups)
    units = units_of(parts)
    pairs = [scatter_pair(u, m, l, parts, pair_buf, scatter_sems, groups) for u, (m, l) in enumerate(units)]
    lines, sent, forwards = {}, {}, {}
    lag_sum, lag_forward = 1, 3
    for tick in range(len(units) + lag_forward):
        if tick < len(units):
            m, l = units[tick]
            lines[tick] = scatter_line(
                tick, m, l, parts, pair_buf, line_buf, pairs[tick], scatter_sems, groups
            )
        u = tick - lag_sum
        if 0 <= u < len(units):
            m, l = units[u]
            own[m][l] = scatter_sum(m, l, pair_buf, line_buf, lines[u], groups)
            sent[u] = gather_one(groups, u, m, l, own, full, gather_sems)
            if adam:
                moment, variance, direction = adam_direction(means[m][l], squares[m][l], own[m][l])
                moments[m][l] = moment
                variances[m][l] = variance
                directions[m][l] = direction
        u = tick - lag_forward
        if 0 <= u < len(units):
            m, l = units[u]
            forwards[u] = gather_forward(groups, u, m, l, full, gather_sems)
    for u, (m, l) in enumerate(units):
        gather_finish(groups, u, m, l, full, gather_sems, sent[u], forwards[u])
        pairs[u].wait_send()
        for copy in lines[u]:
            copy.wait_send()


def gather_sem_shapes(units, groups):
    return [pltpu.SemaphoreType.DMA((units, groups))] * 4


def reduce_call(parts, means, squares, shard, collective):
    groups = shard // 2
    count = len(parts)
    adam = means is not None
    layers, rank, _ = parts[0].shape
    rows = rank // shard
    parts = [p.reshape(layers, groups, 2, rows, p.shape[2]) for p in parts]
    widths = [p.shape[4] for p in parts]
    units = count * layers
    vmem = pl.BlockSpec(memory_space=pltpu.VMEM)
    full = [jax.ShapeDtypeStruct(p.shape, p.dtype) for p in parts]
    small = [jax.ShapeDtypeStruct((layers, rows, w), jnp.float32) for w in widths]
    outs = full + (small * 3 if adam else [])
    args = list(parts) + (list(means) + list(squares) if adam else [])
    result = pl.pallas_call(
        functools.partial(reduce_kernel, groups, count, adam),
        out_shape=outs,
        in_specs=[vmem] * len(args),
        out_specs=[vmem] * len(outs),
        scratch_shapes=[pltpu.VMEM((layers, rows, w), jnp.float32) for w in widths]
        + [pltpu.VMEM((layers, groups, rows, w), jnp.float32) for w in widths]
        + [pltpu.VMEM((layers, groups - 1, rows, w), jnp.float32) for w in widths]
        + [pltpu.SemaphoreType.DMA((units,))] * 2
        + [pltpu.SemaphoreType.DMA((units, groups))] * 2
        + gather_sem_shapes(units, groups),
        compiler_params=pltpu.CompilerParams(
            collective_id=collective, has_side_effects=True, vmem_limit_bytes=VMEM_LIMIT
        ),
        name="reduce_gather_adam" if adam else "reduce_gather",
    )(*args)
    whole = [r.reshape(layers, rank, r.shape[4]) for r in result[:count]]
    return whole, [result[count * k : count * (k + 1)] for k in range(1, 4 if adam else 1)]


def gather_power_kernel(groups, count, *refs):
    own, powers = refs[:count], refs[count : 2 * count]
    refs = refs[2 * count :]
    full, sums = refs[:count], refs[count : 2 * count]
    refs = refs[2 * count :]
    first, half, second = refs[:count], refs[count : 2 * count], refs[2 * count : 3 * count]
    sems = refs[3 * count :]
    gather_sems = sems[:4]
    send, recv = sems[4:]
    me = lax.axis_index("tensor")
    side = lax.rem(me, 2)
    near = me + 1 - 2 * side
    far = lax.rem(me + 2, 4)
    greet(groups, (near, far))
    for_near = [
        remote(powers[m].at[:, 1 - side], first[m], send.at[0, m], recv.at[0, m], {"tensor": near})
        for m in range(count)
    ]
    for copy in for_near:
        copy.start()
    units = units_of(own)
    sent = [gather_one(groups, u, m, l, own, full, gather_sems) for u, (m, l) in enumerate(units)]
    for_far = []
    for m in range(count):
        for_near[m].wait_recv()
        half[m][...] = powers[m][:, side] + first[m][...]
        copy = remote(half[m], second[m], send.at[1, m], recv.at[1, m], {"tensor": far})
        copy.start()
        for_far.append(copy)
    forwards = [gather_forward(groups, u, m, l, full, gather_sems) for u, (m, l) in enumerate(units)]
    back = []
    for m in range(count):
        for_far[m].wait_recv()
        sums[m][:, side] = half[m][...] + second[m][...]
        copy = remote(
            sums[m].at[:, side], sums[m].at[:, side], send.at[2, m], recv.at[2, m], {"tensor": near}
        )
        copy.start()
        back.append(copy)
    for u, (m, l) in enumerate(units):
        gather_finish(groups, u, m, l, full, gather_sems, sent[u], forwards[u])
    for m in range(count):
        for_near[m].wait_send()
        for_far[m].wait_send()
        back[m].wait_send()
        remote(
            sums[m].at[:, 1 - side],
            sums[m].at[:, 1 - side],
            send.at[2, m],
            recv.at[2, m],
            {"tensor": near},
        ).wait_recv()


def gather_power_call(own, powers, shard, collective):
    groups = shard // 2
    count = len(own)
    layers, rows, _ = own[0].shape
    widths = [o.shape[2] for o in own]
    depth, rank = powers[0].shape[1:]
    powers = [p.reshape(layers, 2, depth // 2, rank) for p in powers]
    units = count * layers
    vmem = pl.BlockSpec(memory_space=pltpu.VMEM)
    outs = [
        jax.ShapeDtypeStruct((layers, groups, 2, rows, w), jnp.float32) for w in widths
    ] + [jax.ShapeDtypeStruct(p.shape, jnp.float32) for p in powers]
    halves = [pltpu.VMEM((layers, depth // 2, rank), jnp.float32) for _ in powers]
    result = pl.pallas_call(
        functools.partial(gather_power_kernel, groups, count),
        out_shape=outs,
        in_specs=[vmem] * (2 * count),
        out_specs=[vmem] * len(outs),
        scratch_shapes=halves * 3
        + gather_sem_shapes(units, groups)
        + [pltpu.SemaphoreType.DMA((3, count))] * 2,
        compiler_params=pltpu.CompilerParams(
            collective_id=collective, has_side_effects=True, vmem_limit_bytes=VMEM_LIMIT
        ),
        name="gather_power",
    )(*own, *powers)
    whole = [r.reshape(layers, 2 * groups * rows, r.shape[4]) for r in result[:count]]
    return whole, [r.reshape(layers, depth, rank) for r in result[count:]]


def mix(left, right):
    return jnp.einsum("lrs,lst->lrt", left, right, precision=highest)


def refresh(gram):
    rank = gram.shape[-1]
    eye = jnp.eye(rank, dtype=jnp.float32)
    total = jnp.sum(gram * eye, axis=(1, 2))
    scale = jnp.sqrt(total) + scale_epsilon
    gram = gram / scale[:, None, None] / scale[:, None, None]
    product = None
    for sweep in range(SWEEPS):
        factor = coeff_linear * eye + coeff_square * gram + coeff_fourth * mix(gram, gram)
        product = factor if product is None else mix(product, factor)
        if sweep + 1 < SWEEPS:
            gram = mix(factor, mix(gram, factor))
    return product, scale


def local(shard, *args):
    gradients, bases, moments_in = args[0:2], args[2:4], args[4:8]
    partial = [
        jnp.einsum("ldr,ldn->lrn", basis, gradient, precision=high)
        for gradient, basis in zip(gradients, bases)
    ]
    flipped = [jnp.transpose(a, (1, 0, 2)) for a in moments_in]
    projected, (moment, variance, direction) = reduce_call(
        partial, flipped[0::2], flipped[1::2], shard, 1
    )
    partial_power = [
        jnp.einsum("ldn,lrn->ldr", gradient, rows, precision=high)
        for gradient, rows in zip(gradients, projected)
    ]
    directions, power = gather_power_call(direction, partial_power, shard, 2)
    grams = jnp.concatenate(
        [jnp.einsum("ldr,lds->lrs", p, p, precision=highest) for p in power], axis=2
    )
    (grams,), _ = reduce_call([grams], None, None, shard, 3)
    rank = grams.shape[1]
    layers = grams.shape[0]
    stacked = jnp.concatenate([grams[:, :, :rank], grams[:, :, rank:]], axis=0)
    factors, scale = refresh(stacked)
    updates = [
        jnp.einsum("ldr,lrn->ldn", basis, rows, precision=high)
        for basis, rows in zip(bases, directions)
    ]
    refreshed = [
        jnp.einsum(
            "ldr,lrs->lds",
            p / scale[layers * m : layers * (m + 1), None, None],
            factors[layers * m : layers * (m + 1)],
            precision=highest,
        )
        for m, p in enumerate(power)
    ]
    back = [jnp.transpose(a, (1, 0, 2)) for pair in zip(moment, variance) for a in pair]
    return (*updates, *back, *refreshed)


def solution(mesh):
    wide, low, basis = P(None, "shard", "tensor"), P("shard", None, "tensor"), P(None, "shard", None)
    return jax.shard_map(
        functools.partial(local, mesh.shape["shard"]),
        mesh=mesh,
        in_specs=(wide, wide, basis, basis, low, low, low, low),
        out_specs=(wide, wide, low, low, low, low, basis, basis),
        check_vma=False,
    )
```

```python
import functools

import jax
import jax.numpy as jnp
from jax import lax
from jax.experimental import pallas as pl
from jax.experimental.pallas import tpu as pltpu
from jax.sharding import PartitionSpec as P

SWEEPS = 3
ADAM_STEP = 10

high = lax.Precision.HIGH
highest = lax.Precision.HIGHEST
coeff_linear = 3.4445
coeff_square = -4.775
coeff_fourth = 2.0315
scale_epsilon = 1e-06
adam_epsilon = 1e-08
beta_first = 0.9
beta_second = 0.99

MESH = pl.DeviceIdType.MESH
VMEM_LIMIT = 56 * 2**20


def adam_direction(mean, square, projected):
    moment = beta_first * mean + (1.0 - beta_first) * projected
    variance = beta_second * square + (1.0 - beta_second) * projected * projected
    corrected = moment / (1.0 - beta_first**ADAM_STEP)
    spread = jnp.sqrt(variance / (1.0 - beta_second**ADAM_STEP)) + adam_epsilon
    return (moment, variance, corrected / spread)


def remote(src, dst, send, recv, device):
    return pltpu.make_async_remote_copy(
        src_ref=src,
        dst_ref=dst,
        send_sem=send,
        recv_sem=recv,
        device_id=device,
        device_id_type=MESH,
    )


def place():
    me = lax.axis_index("shard")
    return me // 2, lax.rem(me, 2)


def greet(groups, tensor_peers=()):
    line, side = place()
    barrier = pltpu.get_barrier_semaphore()
    devices = [right_of(groups), left_of(groups), pair_of()]
    devices.extend({"tensor": other} for other in tensor_peers)
    for device in devices:
        pl.semaphore_signal(barrier, inc=1, device_id=device, device_id_type=MESH)
    pl.semaphore_wait(barrier, len(devices))


def right_of(groups):
    line, side = place()
    return {"shard": lax.rem(line + 1, groups) * 2 + side}


def left_of(groups):
    line, side = place()
    return {"shard": lax.rem(line + groups - 1, groups) * 2 + side}


def pair_of():
    line, side = place()
    return {"shard": line * 2 + 1 - side}


def units_of(refs):
    return [(which, layer) for layer in range(refs[0].shape[0]) for which in range(len(refs))]


class Gather:
    def __init__(self, groups, own, full, sems):
        self.groups, self.own, self.full, self.sems = groups, own, full, sems
        self.units = units_of(own)
        self.started = []

    def send(self, u):
        m, l = self.units[u]
        line, side = place()
        zs, zr, xs, xr = self.sems
        source, target = self.own[m].at[l], self.full[m].at[l, line, side]
        ahead = remote(source, target, zs.at[u, 1], zr.at[u, 1], right_of(self.groups))
        ahead.start()
        pair = remote(source, target, xs.at[u, 0], xr.at[u, 0], pair_of())
        pair.start()
        self.full[m][l, line, side] = self.own[m][l]
        self.started += [ahead, pair]

    def hop(self, u, step):
        m, l = self.units[u]
        line, side = place()
        zs, zr, xs, xr = self.sems
        block = self.full[m].at[l, lax.rem(line + self.groups - step, self.groups), side]
        remote(block, block, zs.at[u, step], zr.at[u, step], right_of(self.groups)).wait_recv()
        if step + 1 < self.groups:
            ahead = remote(
                block, block, zs.at[u, step + 1], zr.at[u, step + 1], right_of(self.groups)
            )
            ahead.start()
            self.started.append(ahead)
        pair = remote(block, block, xs.at[u, step], xr.at[u, step], pair_of())
        pair.start()
        self.started.append(pair)

    def landed(self, u):
        m, l = self.units[u]
        line, side = place()
        zs, zr, xs, xr = self.sems
        for step in range(self.groups):
            source = lax.rem(line + self.groups - step, self.groups)
            block = self.full[m].at[l, source, 1 - side]
            remote(block, block, xs.at[u, step], xr.at[u, step], pair_of()).wait_recv()

    def drain(self):
        for copy in self.started:
            copy.wait_send()


class Scatter:
    def __init__(self, groups, parts, pair_buf, line_buf, own, sems):
        self.groups, self.parts, self.own, self.sems = groups, parts, own, sems
        self.pair_buf, self.line_buf = pair_buf, line_buf
        self.units = units_of(parts)
        self.started = []
        self.pairs = {}

    def send(self, u):
        m, l = self.units[u]
        line, side = place()
        copy = remote(
            self.parts[m].at[l, :, 1 - side],
            self.pair_buf[m].at[l],
            self.sems[0].at[u],
            self.sems[1].at[u],
            pair_of(),
        )
        copy.start()
        self.pairs[u] = copy
        self.started.append(copy)

    def ahead(self, u, step, block):
        m, l = self.units[u]
        copy = remote(
            block,
            self.line_buf[m].at[l, step - 1],
            self.sems[2].at[u, step],
            self.sems[3].at[u, step],
            right_of(self.groups),
        )
        copy.start()
        self.started.append(copy)

    def pair(self, u):
        m, l = self.units[u]
        line, side = place()
        self.pairs[u].wait_recv()
        held, part = self.pair_buf[m], self.parts[m]
        first = lax.rem(line + self.groups - 1, self.groups)
        held[l, first] = held[l, first] + part[l, first, side]
        self.ahead(u, 1, held.at[l, first])
        for step in range(1, self.groups):
            g = lax.rem(line + 2 * self.groups - 1 - step, self.groups)
            held[l, g] = held[l, g] + part[l, g, side]

    def hop(self, u, step):
        m, l = self.units[u]
        line, side = place()
        buf = self.line_buf[m]
        block = buf.at[l, step - 1]
        remote(
            block, block, self.sems[2].at[u, step], self.sems[3].at[u, step], right_of(self.groups)
        ).wait_recv()
        g = lax.rem(line + 2 * self.groups - 1 - step, self.groups)
        total = buf[l, step - 1] + self.pair_buf[m][l, g]
        if step + 1 < self.groups:
            buf[l, step - 1] = total
            self.ahead(u, step + 1, block)
        else:
            self.own[m][l] = total

    def drain(self):
        for copy in self.started:
            copy.wait_send()


def reduce_events(scatter, gather, sizes, begin, delay, finish=None):
    events = []
    groups = scatter.groups
    clock = begin
    for u in range(len(scatter.units)):
        clock += sizes[u]
        events.append((clock, functools.partial(scatter.pair, u)))
        for step in range(1, groups):
            events.append((clock + delay * step, functools.partial(scatter.hop, u, step)))
        ready = clock + delay * (groups - 1)
        events.append((ready, functools.partial(gather.send, u)))
        if finish is not None:
            events.append((ready, functools.partial(finish, u)))
        for step in range(1, groups):
            events.append((ready + delay * step, functools.partial(gather.hop, u, step)))
    return events


def play(events):
    for _, action in sorted(events, key=lambda event: event[0]):
        action()


def reduce_kernel(groups, count, *refs):
    def take():
        nonlocal refs
        head, refs = refs[:count], refs[count:]
        return head

    parts, means, squares = take(), take(), take()
    full, moments, variances, directions = take(), take(), take(), take()
    own, pair_buf, line_buf = take(), take(), take()
    scatter = Scatter(groups, parts, pair_buf, line_buf, own, refs[:4])
    gather = Gather(groups, own, full, refs[4:])
    greet(groups)
    for u in range(len(scatter.units)):
        scatter.send(u)

    def adam(u):
        m, l = scatter.units[u]
        moment, variance, direction = adam_direction(means[m][l], squares[m][l], own[m][l])
        moments[m][l] = moment
        variances[m][l] = variance
        directions[m][l] = direction

    most = max(p.shape[-1] for p in parts)
    sizes = [16.0 * parts[m].shape[-1] / most for m, _ in scatter.units]
    play(reduce_events(scatter, gather, sizes, 0.0, 6.0, adam))
    for u in range(len(scatter.units)):
        gather.landed(u)
    scatter.drain()
    gather.drain()


def reduce_scratch(layers, groups, rows, widths):
    return (
        [pltpu.VMEM((layers, rows, w), jnp.float32) for w in widths]
        + [pltpu.VMEM((layers, groups, rows, w), jnp.float32) for w in widths]
        + [pltpu.VMEM((layers, groups - 1, rows, w), jnp.float32) for w in widths]
    )


def scatter_sems(units, groups):
    return [pltpu.SemaphoreType.DMA((units,))] * 2 + [pltpu.SemaphoreType.DMA((units, groups))] * 2


def gather_sems(units, groups):
    return [pltpu.SemaphoreType.DMA((units, groups))] * 4


def reduce_call(parts, means, squares, shard, collective):
    groups = shard // 2
    count = len(parts)
    layers, rank, _ = parts[0].shape
    rows = rank // shard
    parts = [p.reshape(layers, groups, 2, rows, p.shape[2]) for p in parts]
    widths = [p.shape[4] for p in parts]
    units = count * layers
    vmem = pl.BlockSpec(memory_space=pltpu.VMEM)
    outs = [jax.ShapeDtypeStruct(p.shape, p.dtype) for p in parts]
    outs += [jax.ShapeDtypeStruct((layers, rows, w), jnp.float32) for w in widths] * 3
    result = pl.pallas_call(
        functools.partial(reduce_kernel, groups, count),
        out_shape=outs,
        in_specs=[vmem] * (3 * count),
        out_specs=[vmem] * len(outs),
        scratch_shapes=reduce_scratch(layers, groups, rows, widths)
        + scatter_sems(units, groups)
        + gather_sems(units, groups),
        compiler_params=pltpu.CompilerParams(
            collective_id=collective, has_side_effects=True, vmem_limit_bytes=VMEM_LIMIT
        ),
        name="reduce_gather_adam",
    )(*parts, *means, *squares)
    whole = [r.reshape(layers, rank, r.shape[4]) for r in result[:count]]
    return whole, [result[count * k : count * (k + 1)] for k in range(1, 4)]


def mix(left, right):
    return jnp.dot(left, right, precision=highest, preferred_element_type=jnp.float32)


def refresh(gram):
    rank = gram.shape[-1]
    eye = (
        lax.broadcasted_iota(jnp.int32, (rank, rank), 0)
        == lax.broadcasted_iota(jnp.int32, (rank, rank), 1)
    ).astype(jnp.float32)
    total = jnp.sum(jnp.sum(gram * eye, axis=0, keepdims=True), axis=1, keepdims=True)
    scale = jnp.sqrt(total) + scale_epsilon
    gram = gram / scale / scale
    product = None
    for sweep in range(SWEEPS):
        factor = coeff_linear * eye + coeff_square * gram + coeff_fourth * mix(gram, gram)
        product = factor if product is None else mix(product, factor)
        if sweep + 1 < SWEEPS:
            gram = mix(factor, mix(gram, factor))
    return product, scale


def refresh_kernel(groups, count, *refs):
    def take():
        nonlocal refs
        head, refs = refs[:count], refs[count:]
        return head

    own, powers, full, refreshed = take(), take(), take(), take()
    first, half, second, sums = take(), take(), take(), take()
    grams, gram_full = take(), take()
    gram_own, pair_buf, line_buf = take(), take(), take()
    gather = Gather(groups, own, full, refs[:4])
    scatter = Scatter(groups, grams, pair_buf, line_buf, gram_own, refs[4:8])
    gram_gather = Gather(groups, gram_own, gram_full, refs[8:12])
    send, recv = refs[12:]
    layers, _, depth, rank = powers[0].shape
    me = lax.axis_index("tensor")
    side = lax.rem(me, 2)
    near, far = me + 1 - 2 * side, lax.rem(me + 2, 4)
    greet(groups, (near, far))
    tensor_copies = []

    def exchange(stage, m, src, dst, device):
        copy = remote(src, dst, send.at[stage, m], recv.at[stage, m], {"tensor": device})
        copy.start()
        tensor_copies.append(copy)
        return copy

    to_near = [
        exchange(0, m, powers[m].at[:, 1 - side], first[m], near) for m in range(count)
    ]
    units = len(gather.units)
    for u in range(units):
        gather.send(u)
    to_far = []
    for m in range(count):
        to_near[m].wait_recv()
        half[m][...] = powers[m][:, side] + first[m][...]
        to_far.append(exchange(1, m, half[m], second[m], far))
    for u in range(units):
        gather.hop(u, 1)
    for m in range(count):
        to_far[m].wait_recv()
        sums[m][:, side] = half[m][...] + second[m][...]
        exchange(2, m, sums[m].at[:, side], sums[m].at[:, side], near)
    for m in range(count):
        other = sums[m].at[:, 1 - side]
        remote(other, other, send.at[2, m], recv.at[2, m], {"tensor": near}).wait_recv()
    for u, (m, l) in enumerate(scatter.units):
        lower, upper = sums[m][l, 0], sums[m][l, 1]
        gram = lax.dot_general(
            lower, lower, (((0,), (0,)), ((), ())), precision=highest,
            preferred_element_type=jnp.float32,
        ) + lax.dot_general(
            upper, upper, (((0,), (0,)), ((), ())), precision=highest,
            preferred_element_type=jnp.float32,
        )
        grams[m][l] = gram.reshape(grams[m].shape[1:])
        scatter.send(u)
    events = reduce_events(scatter, gram_gather, [2.0] * units, 0.0, 4.0)
    for step in range(2, groups):
        for u in range(units):
            at = (step - 2) * 18.0 + 18.0 * (u + 1) / units
            events.append((at, functools.partial(gather.hop, u, step)))
    play(events)
    for u, (m, l) in enumerate(scatter.units):
        gram_gather.landed(u)
    for m in range(count):

        def one(l, carry, m=m):
            factor, scale = refresh(gram_full[m][l].reshape(rank, rank))
            for part in range(2):
                refreshed[m][l, part] = mix(sums[m][l, part] / scale, factor)
            return carry

        lax.fori_loop(0, layers, one, 0)
    for u in range(units):
        gather.landed(u)
    for copy in tensor_copies:
        copy.wait_send()
    scatter.drain()
    gram_gather.drain()
    gather.drain()


def refresh_call(own, powers, shard, collective):
    groups = shard // 2
    count = len(own)
    layers, rows, _ = own[0].shape
    widths = [o.shape[2] for o in own]
    depth, rank = powers[0].shape[1:]
    powers = [p.reshape(layers, 2, depth // 2, rank) for p in powers]
    units = count * layers
    vmem = pl.BlockSpec(memory_space=pltpu.VMEM)
    outs = [
        jax.ShapeDtypeStruct((layers, groups, 2, rows, w), jnp.float32) for w in widths
    ] + [jax.ShapeDtypeStruct(p.shape, jnp.float32) for p in powers]
    halves = [pltpu.VMEM((layers, depth // 2, rank), jnp.float32)] * count
    sums = [pltpu.VMEM((layers, 2, depth // 2, rank), jnp.float32)] * count
    squares = [pltpu.VMEM((layers, groups, 2, rows, rank), jnp.float32)] * count
    result = pl.pallas_call(
        functools.partial(refresh_kernel, groups, count),
        out_shape=outs,
        in_specs=[vmem] * (2 * count),
        out_specs=[vmem] * len(outs),
        scratch_shapes=halves * 3
        + sums
        + squares * 2
        + reduce_scratch(layers, groups, rows, [rank] * count)
        + gather_sems(units, groups)
        + scatter_sems(units, groups)
        + gather_sems(units, groups)
        + [pltpu.SemaphoreType.DMA((3, count))] * 2,
        compiler_params=pltpu.CompilerParams(
            collective_id=collective, has_side_effects=True, vmem_limit_bytes=VMEM_LIMIT
        ),
        name="gather_refresh",
    )(*own, *powers)
    whole = [r.reshape(layers, rank, r.shape[4]) for r in result[:count]]
    return whole, [r.reshape(layers, depth, rank) for r in result[count:]]


def local(shard, *args):
    gradients, bases, moments_in = args[0:2], args[2:4], args[4:8]
    partial = [
        jnp.einsum("ldr,ldn->lrn", basis, gradient, precision=high)
        for gradient, basis in zip(gradients, bases)
    ]
    flipped = [jnp.transpose(a, (1, 0, 2)) for a in moments_in]
    projected, (moment, variance, direction) = reduce_call(
        partial, flipped[0::2], flipped[1::2], shard, 1
    )
    partial_power = [
        jnp.einsum("ldn,lrn->ldr", gradient, rows, precision=high)
        for gradient, rows in zip(gradients, projected)
    ]
    directions, refreshed = refresh_call(direction, partial_power, shard, 2)
    updates = [
        jnp.einsum("ldr,lrn->ldn", basis, rows, precision=high)
        for basis, rows in zip(bases, directions)
    ]
    back = [jnp.transpose(a, (1, 0, 2)) for pair in zip(moment, variance) for a in pair]
    return (*updates, *back, *refreshed)


def solution(mesh):
    wide, low, basis = P(None, "shard", "tensor"), P("shard", None, "tensor"), P(None, "shard", None)
    return jax.shard_map(
        functools.partial(local, mesh.shape["shard"]),
        mesh=mesh,
        in_specs=(wide, wide, basis, basis, low, low, low, low),
        out_specs=(wide, wide, low, low, low, low, basis, basis),
        check_vma=False,
    )
```

```python
import functools

import jax
import jax.numpy as jnp
from jax import lax
from jax.experimental import pallas as pl
from jax.experimental.pallas import tpu as pltpu
from jax.sharding import PartitionSpec as P

SWEEPS = 3
ADAM_STEP = 10

high = lax.Precision.HIGH
highest = lax.Precision.HIGHEST
coeff_linear = 3.4445
coeff_square = -4.775
coeff_fourth = 2.0315
scale_epsilon = 1e-06
adam_epsilon = 1e-08
beta_first = 0.9
beta_second = 0.99

MESH = pl.DeviceIdType.MESH
VMEM_LIMIT = 56 * 2**20


def adam_direction(mean, square, projected):
    moment = beta_first * mean + (1.0 - beta_first) * projected
    variance = beta_second * square + (1.0 - beta_second) * projected * projected
    corrected = moment / (1.0 - beta_first**ADAM_STEP)
    spread = jnp.sqrt(variance / (1.0 - beta_second**ADAM_STEP)) + adam_epsilon
    return (moment, variance, corrected / spread)


def remote(src, dst, send, recv, device):
    return pltpu.make_async_remote_copy(
        src_ref=src,
        dst_ref=dst,
        send_sem=send,
        recv_sem=recv,
        device_id=device,
        device_id_type=MESH,
    )


def place():
    me = lax.axis_index("shard")
    return me // 2, lax.rem(me, 2)


def greet(groups, tensor_peers=()):
    line, side = place()
    barrier = pltpu.get_barrier_semaphore()
    devices = [right_of(groups), left_of(groups), pair_of()]
    devices.extend({"tensor": other} for other in tensor_peers)
    for device in devices:
        pl.semaphore_signal(barrier, inc=1, device_id=device, device_id_type=MESH)
    pl.semaphore_wait(barrier, len(devices))


def right_of(groups):
    line, side = place()
    return {"shard": lax.rem(line + 1, groups) * 2 + side}


def left_of(groups):
    line, side = place()
    return {"shard": lax.rem(line + groups - 1, groups) * 2 + side}


def pair_of():
    line, side = place()
    return {"shard": line * 2 + 1 - side}


def units_of(refs):
    return [(which, layer) for layer in range(refs[0].shape[0]) for which in range(len(refs))]


class Gather:
    def __init__(self, groups, own, full, sems, early=()):
        self.groups, self.own, self.full, self.sems = groups, own, full, sems
        self.units = units_of(own)
        self.early = early
        self.started = []

    def to_pair(self, u, step, source, target):
        _, _, xs, xr = self.sems
        copy = remote(source, target, xs.at[u, step], xr.at[u, step], pair_of())
        copy.start()
        self.started.append(copy)

    def ahead(self, u, step, source, target):
        zs, zr, _, _ = self.sems
        copy = remote(source, target, zs.at[u, step], zr.at[u, step], right_of(self.groups))
        copy.start()
        self.started.append(copy)

    def send(self, u):
        m, l = self.units[u]
        line, side = place()
        source, target = self.own[m].at[l], self.full[m].at[l, line, side]
        if (m, l) not in self.early:
            self.ahead(u, 1, source, target)
        self.to_pair(u, 0, source, target)
        self.full[m][l, line, side] = self.own[m][l]

    def from_pair(self, u, step):
        m, l = self.units[u]
        line, side = place()
        _, _, xs, xr = self.sems
        source = lax.rem(line + self.groups - step, self.groups)
        block = self.full[m].at[l, source, 1 - side]
        remote(block, block, xs.at[u, step], xr.at[u, step], pair_of()).wait_recv()

    def turn(self, u):
        m, l = self.units[u]
        if (m, l) in self.early:
            line, _ = place()
            self.from_pair(u, 0)
            block = self.full[m].at[l, line]
            self.ahead(u, 1, block, block)

    def hop(self, u, step):
        m, l = self.units[u]
        line, side = place()
        zs, zr, _, _ = self.sems
        early = (m, l) in self.early
        source = lax.rem(line + self.groups - step, self.groups)
        block = self.full[m].at[l, source] if early else self.full[m].at[l, source, side]
        remote(block, block, zs.at[u, step], zr.at[u, step], right_of(self.groups)).wait_recv()
        if step + 1 < self.groups:
            self.ahead(u, step + 1, block, block)
        if not early:
            self.to_pair(u, step, block, block)

    def landed(self, u):
        if self.units[u] not in self.early:
            for step in range(self.groups):
                self.from_pair(u, step)

    def drain(self):
        for copy in self.started:
            copy.wait_send()


class Scatter:
    def __init__(self, groups, parts, pair_buf, line_buf, own, sems):
        self.groups, self.parts, self.own, self.sems = groups, parts, own, sems
        self.pair_buf, self.line_buf = pair_buf, line_buf
        self.units = units_of(parts)
        self.started = []
        self.pairs = {}

    def send(self, u):
        m, l = self.units[u]
        line, side = place()
        copy = remote(
            self.parts[m].at[l, :, 1 - side],
            self.pair_buf[m].at[l],
            self.sems[0].at[u],
            self.sems[1].at[u],
            pair_of(),
        )
        copy.start()
        self.pairs[u] = copy
        self.started.append(copy)

    def ahead(self, u, step, block):
        m, l = self.units[u]
        copy = remote(
            block,
            self.line_buf[m].at[l, step - 1],
            self.sems[2].at[u, step],
            self.sems[3].at[u, step],
            right_of(self.groups),
        )
        copy.start()
        self.started.append(copy)

    def pair(self, u):
        m, l = self.units[u]
        line, side = place()
        self.pairs[u].wait_recv()
        held, part = self.pair_buf[m], self.parts[m]
        first = lax.rem(line + self.groups - 1, self.groups)
        held[l, first] = held[l, first] + part[l, first, side]
        self.ahead(u, 1, held.at[l, first])
        for step in range(1, self.groups):
            g = lax.rem(line + 2 * self.groups - 1 - step, self.groups)
            held[l, g] = held[l, g] + part[l, g, side]

    def hop(self, u, step):
        m, l = self.units[u]
        line, side = place()
        buf = self.line_buf[m]
        block = buf.at[l, step - 1]
        remote(
            block, block, self.sems[2].at[u, step], self.sems[3].at[u, step], right_of(self.groups)
        ).wait_recv()
        g = lax.rem(line + 2 * self.groups - 1 - step, self.groups)
        total = buf[l, step - 1] + self.pair_buf[m][l, g]
        if step + 1 < self.groups:
            buf[l, step - 1] = total
            self.ahead(u, step + 1, block)
        else:
            self.own[m][l] = total

    def drain(self):
        for copy in self.started:
            copy.wait_send()


def reduce_events(scatter, gather, sizes, begin, delay, finish=None):
    events = []
    groups = scatter.groups
    clock = begin
    for u in range(len(scatter.units)):
        clock += sizes[u]
        events.append((clock, functools.partial(scatter.pair, u)))
        for step in range(1, groups):
            events.append((clock + delay * step, functools.partial(scatter.hop, u, step)))
        ready = clock + delay * (groups - 1)
        events.append((ready, functools.partial(gather.send, u)))
        events.append((ready + delay * 0.5, functools.partial(gather.turn, u)))
        if finish is not None:
            events.append((ready, functools.partial(finish, u)))
        for step in range(1, groups):
            events.append((ready + delay * step, functools.partial(gather.hop, u, step)))
    return events


def play(events):
    for _, action in sorted(events, key=lambda event: event[0]):
        action()


def reduce_kernel(groups, count, *refs):
    def take():
        nonlocal refs
        head, refs = refs[:count], refs[count:]
        return head

    parts, means, squares = take(), take(), take()
    full, moments, variances, directions = take(), take(), take(), take()
    own, pair_buf, line_buf = take(), take(), take()
    scatter = Scatter(groups, parts, pair_buf, line_buf, own, refs[:4])
    gather = Gather(groups, own, full, refs[4:], ((count - 1, 0),))
    greet(groups)
    for u in range(len(scatter.units)):
        scatter.send(u)

    def adam(u):
        m, l = scatter.units[u]
        moment, variance, direction = adam_direction(means[m][l], squares[m][l], own[m][l])
        moments[m][l] = moment
        variances[m][l] = variance
        directions[m][l] = direction

    most = max(p.shape[-1] for p in parts)
    sizes = [16.0 * parts[m].shape[-1] / most for m, _ in scatter.units]
    play(reduce_events(scatter, gather, sizes, 0.0, 6.0, adam))
    for u in range(len(scatter.units)):
        gather.landed(u)
    scatter.drain()
    gather.drain()


def reduce_scratch(layers, groups, rows, widths):
    return (
        [pltpu.VMEM((layers, rows, w), jnp.float32) for w in widths]
        + [pltpu.VMEM((layers, groups, rows, w), jnp.float32) for w in widths]
        + [pltpu.VMEM((layers, groups - 1, rows, w), jnp.float32) for w in widths]
    )


def scatter_sems(units, groups):
    return [pltpu.SemaphoreType.DMA((units,))] * 2 + [pltpu.SemaphoreType.DMA((units, groups))] * 2


def gather_sems(units, groups):
    return [pltpu.SemaphoreType.DMA((units, groups))] * 4


def reduce_call(parts, means, squares, shard, collective):
    groups = shard // 2
    count = len(parts)
    layers, rank, _ = parts[0].shape
    rows = rank // shard
    parts = [p.reshape(layers, groups, 2, rows, p.shape[2]) for p in parts]
    widths = [p.shape[4] for p in parts]
    units = count * layers
    vmem = pl.BlockSpec(memory_space=pltpu.VMEM)
    outs = [jax.ShapeDtypeStruct(p.shape, p.dtype) for p in parts]
    outs += [jax.ShapeDtypeStruct((layers, rows, w), jnp.float32) for w in widths] * 3
    result = pl.pallas_call(
        functools.partial(reduce_kernel, groups, count),
        out_shape=outs,
        in_specs=[vmem] * (3 * count),
        out_specs=[vmem] * len(outs),
        scratch_shapes=reduce_scratch(layers, groups, rows, widths)
        + scatter_sems(units, groups)
        + gather_sems(units, groups),
        compiler_params=pltpu.CompilerParams(
            collective_id=collective, has_side_effects=True, vmem_limit_bytes=VMEM_LIMIT
        ),
        name="reduce_gather_adam",
    )(*parts, *means, *squares)
    whole = [r.reshape(layers, rank, r.shape[4]) for r in result[:count]]
    return whole, [result[count * k : count * (k + 1)] for k in range(1, 4)]


def mix(left, right):
    return jnp.dot(left, right, precision=highest, preferred_element_type=jnp.float32)


def refresh(grams):
    rank = grams[0].shape[-1]
    eye = (
        lax.broadcasted_iota(jnp.int32, (rank, rank), 0)
        == lax.broadcasted_iota(jnp.int32, (rank, rank), 1)
    ).astype(jnp.float32)
    totals = [
        jnp.sum(jnp.sum(g * eye, axis=0, keepdims=True), axis=1, keepdims=True) for g in grams
    ]
    scales = [jnp.sqrt(total) + scale_epsilon for total in totals]
    grams = [g / scale / scale for g, scale in zip(grams, scales)]
    products = None
    for sweep in range(SWEEPS):
        squared = [mix(g, g) for g in grams]
        factors = [
            coeff_linear * eye + coeff_square * g + coeff_fourth * q
            for g, q in zip(grams, squared)
        ]
        if sweep + 1 < SWEEPS:
            grams = [mix(g, f) for g, f in zip(grams, factors)]
            grams = [mix(f, g) for g, f in zip(grams, factors)]
        if products is None:
            products = factors
        else:
            products = [mix(p, f) for p, f in zip(products, factors)]
    return products, scales


def refresh_kernel(groups, count, *refs):
    def take(number):
        nonlocal refs
        head, refs = refs[:number], refs[number:]
        return head

    own, (powers,), full, (refreshed,) = take(count), take(1), take(count), take(1)
    first, half, second, sums = take(4)
    grams, gram_full = take(1), take(1)
    gram_own, pair_buf, line_buf = take(1), take(1), take(1)
    gather = Gather(groups, own, full, refs[:4], ((count - 1, 0),))
    scatter = Scatter(groups, grams, pair_buf, line_buf, gram_own, refs[4:8])
    gram_gather = Gather(groups, gram_own, gram_full, refs[8:12])
    send, recv = refs[12:]
    layers, rank = powers.shape[1], powers.shape[4]
    me = lax.axis_index("tensor")
    side, mine = lax.rem(me, 2), me // 2
    near, far = me + 1 - 2 * side, lax.rem(me + 2, 4)
    greet(groups, (near, far))
    tensor_copies = []

    def exchange(stage, src, dst, device):
        copy = remote(src, dst, send.at[stage], recv.at[stage], {"tensor": device})
        copy.start()
        tensor_copies.append(copy)
        return copy

    def arrived(stage, block, device):
        remote(block, block, send.at[stage], recv.at[stage], {"tensor": device}).wait_recv()

    far_near = exchange(0, powers.at[1 - mine, :, 1 - side], first.at[1 - mine], near)
    own_near = exchange(1, powers.at[mine, :, 1 - side], first.at[mine], near)
    units = len(gather.units)
    for u in range(units):
        gather.send(u)
    far_near.wait_recv()
    half[1 - mine] = powers[1 - mine, :, side] + first[1 - mine]
    to_far = exchange(2, half.at[1 - mine], second, far)
    own_near.wait_recv()
    half[mine] = powers[mine, :, side] + first[mine]
    for u in range(units):
        gather.turn(u)
    to_far.wait_recv()
    low, high_part = half[mine], second[...]
    sums[:, side] = low + high_part
    exchange(3, sums.at[:, side], sums.at[:, side], near)
    for u in range(units):
        if u < 2:
            gather.hop(u, 1)
    arrived(3, sums.at[:, 1 - side], near)
    for l in range(layers):
        lower, upper = sums[l, 0], sums[l, 1]
        gram = lax.dot_general(
            lower, lower, (((0,), (0,)), ((), ())), precision=highest,
            preferred_element_type=jnp.float32,
        ) + lax.dot_general(
            upper, upper, (((0,), (0,)), ((), ())), precision=highest,
            preferred_element_type=jnp.float32,
        )
        grams[0][l] = gram.reshape(grams[0].shape[1:])
        scatter.send(l)
    events = reduce_events(scatter, gram_gather, [2.0] * layers, 0.0, 3.0)
    for step in range(1, groups):
        for u in range(units):
            if step > 1 or u >= 2:
                at = (step - 2) * 18.0 + 18.0 * (u + 1) / units
                events.append((at, functools.partial(gather.hop, u, step)))
    play(events)
    for u in range(layers):
        gram_gather.landed(u)
    factors, scales = refresh([gram_full[0][l].reshape(rank, rank) for l in range(layers)])
    for l in range(layers):
        refreshed[mine, l, side] = mix(sums[l, side] / scales[l], factors[l])
    block = refreshed.at[mine, :, side]
    exchange(4, block, block, far)
    exchange(5, block, block, near)
    other = refreshed.at[1 - mine, :, side]
    arrived(4, other, far)
    exchange(6, other, other, near)
    for u in range(units):
        gather.landed(u)
    arrived(5, refreshed.at[mine, :, 1 - side], near)
    arrived(6, refreshed.at[1 - mine, :, 1 - side], near)
    for copy in tensor_copies:
        copy.wait_send()
    scatter.drain()
    gram_gather.drain()
    gather.drain()


def refresh_call(own, powers, shard, collective):
    groups = shard // 2
    count = len(own)
    layers, rows, _ = own[0].shape
    widths = [o.shape[2] for o in own]
    depth, rank = powers[0].shape[1:]
    powers = jnp.stack(powers).reshape(count, layers, 2, depth // 2, rank)
    units = count * layers
    vmem = pl.BlockSpec(memory_space=pltpu.VMEM)
    outs = [
        jax.ShapeDtypeStruct((layers, groups, 2, rows, w), jnp.float32) for w in widths
    ] + [jax.ShapeDtypeStruct(powers.shape, jnp.float32)]
    result = pl.pallas_call(
        functools.partial(refresh_kernel, groups, count),
        out_shape=outs,
        in_specs=[vmem] * (count + 1),
        out_specs=[vmem] * len(outs),
        scratch_shapes=[pltpu.VMEM((count, layers, depth // 2, rank), jnp.float32)] * 2
        + [pltpu.VMEM((layers, depth // 2, rank), jnp.float32)]
        + [pltpu.VMEM((layers, 2, depth // 2, rank), jnp.float32)]
        + [pltpu.VMEM((layers, groups, 2, rows, rank), jnp.float32)] * 2
        + reduce_scratch(layers, groups, rows, [rank])
        + gather_sems(units, groups)
        + scatter_sems(layers, groups)
        + gather_sems(layers, groups)
        + [pltpu.SemaphoreType.DMA((7,))] * 2,
        compiler_params=pltpu.CompilerParams(
            collective_id=collective, has_side_effects=True, vmem_limit_bytes=VMEM_LIMIT
        ),
        name="gather_refresh",
    )(*own, powers)
    whole = [r.reshape(layers, rank, r.shape[4]) for r in result[:count]]
    return whole, [r.reshape(layers, depth, rank) for r in result[count]]


def local(shard, *args):
    gradients, bases, moments_in = args[0:2], args[2:4], args[4:8]
    partial = [
        jnp.einsum("ldr,ldn->lrn", basis, gradient, precision=high)
        for gradient, basis in zip(gradients, bases)
    ]
    flipped = [jnp.transpose(a, (1, 0, 2)) for a in moments_in]
    projected, (moment, variance, direction) = reduce_call(
        partial, flipped[0::2], flipped[1::2], shard, 1
    )
    partial_power = [
        jnp.einsum("ldn,lrn->ldr", gradient, rows, precision=high)
        for gradient, rows in zip(gradients, projected)
    ]
    directions, refreshed = refresh_call(direction, partial_power, shard, 2)
    updates = [
        jnp.einsum("ldr,lrn->ldn", basis, rows, precision=high)
        for basis, rows in zip(bases, directions)
    ]
    back = [jnp.transpose(a, (1, 0, 2)) for pair in zip(moment, variance) for a in pair]
    return (*updates, *back, *refreshed)


def solution(mesh):
    wide, low, basis = P(None, "shard", "tensor"), P("shard", None, "tensor"), P(None, "shard", None)
    return jax.shard_map(
        functools.partial(local, mesh.shape["shard"]),
        mesh=mesh,
        in_specs=(wide, wide, basis, basis, low, low, low, low),
        out_specs=(wide, wide, low, low, low, low, basis, basis),
        check_vma=False,
    )
```

```python
import functools

import jax
import jax.numpy as jnp
from jax import lax
from jax.experimental import pallas as pl
from jax.experimental.pallas import tpu as pltpu
from jax.sharding import PartitionSpec as P

SWEEPS = 3
ADAM_STEP = 10

high = lax.Precision.HIGH
highest = lax.Precision.HIGHEST
coeff_linear = 3.4445
coeff_square = -4.775
coeff_fourth = 2.0315
scale_epsilon = 1e-06
adam_epsilon = 1e-08
beta_first = 0.9
beta_second = 0.99

MESH = pl.DeviceIdType.MESH
VMEM_LIMIT = 56 * 2**20


def adam_direction(mean, square, projected):
    moment = beta_first * mean + (1.0 - beta_first) * projected
    variance = beta_second * square + (1.0 - beta_second) * projected * projected
    corrected = moment / (1.0 - beta_first**ADAM_STEP)
    spread = jnp.sqrt(variance / (1.0 - beta_second**ADAM_STEP)) + adam_epsilon
    return (moment, variance, corrected / spread)


def remote(src, dst, send, recv, device):
    return pltpu.make_async_remote_copy(
        src_ref=src,
        dst_ref=dst,
        send_sem=send,
        recv_sem=recv,
        device_id=device,
        device_id_type=MESH,
    )


def place():
    me = lax.axis_index("shard")
    return me // 2, lax.rem(me, 2)


def greet(groups, tensor_peers=()):
    line, side = place()
    barrier = pltpu.get_barrier_semaphore()
    devices = [right_of(groups), left_of(groups), pair_of()]
    devices.extend({"tensor": other} for other in tensor_peers)
    for device in devices:
        pl.semaphore_signal(barrier, inc=1, device_id=device, device_id_type=MESH)
    pl.semaphore_wait(barrier, len(devices))


def right_of(groups):
    line, side = place()
    return {"shard": lax.rem(line + 1, groups) * 2 + side}


def left_of(groups):
    line, side = place()
    return {"shard": lax.rem(line + groups - 1, groups) * 2 + side}


def pair_of():
    line, side = place()
    return {"shard": line * 2 + 1 - side}


def units_of(refs):
    return [(which, layer) for layer in range(refs[0].shape[0]) for which in range(len(refs))]


class Gather:
    def __init__(self, groups, own, full, sems, early=()):
        self.groups, self.own, self.full, self.sems = groups, own, full, sems
        self.units = units_of(own)
        self.early = early
        self.started = []

    def to_pair(self, u, step, source, target):
        _, _, xs, xr = self.sems
        copy = remote(source, target, xs.at[u, step], xr.at[u, step], pair_of())
        copy.start()
        self.started.append(copy)

    def ahead(self, u, step, source, target):
        zs, zr, _, _ = self.sems
        copy = remote(source, target, zs.at[u, step], zr.at[u, step], right_of(self.groups))
        copy.start()
        self.started.append(copy)

    def send(self, u):
        m, l = self.units[u]
        line, side = place()
        source, target = self.own[m].at[l], self.full[m].at[l, line, side]
        if (m, l) not in self.early:
            self.ahead(u, 1, source, target)
        self.to_pair(u, 0, source, target)
        self.full[m][l, line, side] = self.own[m][l]

    def from_pair(self, u, step):
        m, l = self.units[u]
        line, side = place()
        _, _, xs, xr = self.sems
        source = lax.rem(line + self.groups - step, self.groups)
        block = self.full[m].at[l, source, 1 - side]
        remote(block, block, xs.at[u, step], xr.at[u, step], pair_of()).wait_recv()

    def turn(self, u):
        m, l = self.units[u]
        if (m, l) in self.early:
            line, _ = place()
            self.from_pair(u, 0)
            block = self.full[m].at[l, line]
            self.ahead(u, 1, block, block)

    def hop(self, u, step):
        m, l = self.units[u]
        line, side = place()
        zs, zr, _, _ = self.sems
        early = (m, l) in self.early
        source = lax.rem(line + self.groups - step, self.groups)
        block = self.full[m].at[l, source] if early else self.full[m].at[l, source, side]
        remote(block, block, zs.at[u, step], zr.at[u, step], right_of(self.groups)).wait_recv()
        if step + 1 < self.groups:
            self.ahead(u, step + 1, block, block)
        if not early:
            self.to_pair(u, step, block, block)

    def landed(self, u):
        if self.units[u] not in self.early:
            for step in range(self.groups):
                self.from_pair(u, step)

    def drain(self):
        for copy in self.started:
            copy.wait_send()


class Scatter:
    def __init__(self, groups, parts, pair_buf, line_buf, own, sems):
        self.groups, self.parts, self.own, self.sems = groups, parts, own, sems
        self.pair_buf, self.line_buf = pair_buf, line_buf
        self.units = units_of(parts)
        self.started = []
        self.pairs = {}

    def send(self, u):
        m, l = self.units[u]
        line, side = place()
        copy = remote(
            self.parts[m].at[l, :, 1 - side],
            self.pair_buf[m].at[l],
            self.sems[0].at[u],
            self.sems[1].at[u],
            pair_of(),
        )
        copy.start()
        self.pairs[u] = copy
        self.started.append(copy)

    def ahead(self, u, step, block):
        m, l = self.units[u]
        copy = remote(
            block,
            self.line_buf[m].at[l, step - 1],
            self.sems[2].at[u, step],
            self.sems[3].at[u, step],
            right_of(self.groups),
        )
        copy.start()
        self.started.append(copy)

    def pair(self, u):
        m, l = self.units[u]
        line, side = place()
        self.pairs[u].wait_recv()
        held, part = self.pair_buf[m], self.parts[m]
        first = lax.rem(line + self.groups - 1, self.groups)
        held[l, first] = held[l, first] + part[l, first, side]
        self.ahead(u, 1, held.at[l, first])
        for step in range(1, self.groups):
            g = lax.rem(line + 2 * self.groups - 1 - step, self.groups)
            held[l, g] = held[l, g] + part[l, g, side]

    def hop(self, u, step):
        m, l = self.units[u]
        line, side = place()
        buf = self.line_buf[m]
        block = buf.at[l, step - 1]
        remote(
            block, block, self.sems[2].at[u, step], self.sems[3].at[u, step], right_of(self.groups)
        ).wait_recv()
        g = lax.rem(line + 2 * self.groups - 1 - step, self.groups)
        total = buf[l, step - 1] + self.pair_buf[m][l, g]
        if step + 1 < self.groups:
            buf[l, step - 1] = total
            self.ahead(u, step + 1, block)
        else:
            self.own[m][l] = total

    def drain(self):
        for copy in self.started:
            copy.wait_send()


def reduce_events(scatter, gather, sizes, begin, delay, finish=None):
    events = []
    groups = scatter.groups
    clock = begin
    for u in range(len(scatter.units)):
        clock += sizes[u]
        events.append((clock, functools.partial(scatter.pair, u)))
        for step in range(1, groups):
            events.append((clock + delay * step, functools.partial(scatter.hop, u, step)))
        ready = clock + delay * (groups - 1)
        events.append((ready, functools.partial(gather.send, u)))
        events.append((ready + delay * 0.5, functools.partial(gather.turn, u)))
        if finish is not None:
            events.append((ready, functools.partial(finish, u)))
        for step in range(1, groups):
            events.append((ready + delay * step, functools.partial(gather.hop, u, step)))
    return events


def play(events):
    for _, action in sorted(events, key=lambda event: event[0]):
        action()


def reduce_kernel(groups, count, *refs):
    def take():
        nonlocal refs
        head, refs = refs[:count], refs[count:]
        return head

    parts, means, squares = take(), take(), take()
    full, moments, variances, directions = take(), take(), take(), take()
    own, pair_buf, line_buf = take(), take(), take()
    scatter = Scatter(groups, parts, pair_buf, line_buf, own, refs[:4])
    gather = Gather(groups, own, full, refs[4:])
    greet(groups)
    for u in range(len(scatter.units)):
        scatter.send(u)

    def adam(u):
        m, l = scatter.units[u]
        moment, variance, direction = adam_direction(means[m][l], squares[m][l], own[m][l])
        moments[m][l] = moment
        variances[m][l] = variance
        directions[m][l] = direction

    most = max(p.shape[-1] for p in parts)
    sizes = [16.0 * parts[m].shape[-1] / most for m, _ in scatter.units]
    play(reduce_events(scatter, gather, sizes, 0.0, 6.0, adam))
    for u in range(len(scatter.units)):
        gather.landed(u)
    scatter.drain()
    gather.drain()


def reduce_scratch(layers, groups, rows, widths):
    return (
        [pltpu.VMEM((layers, rows, w), jnp.float32) for w in widths]
        + [pltpu.VMEM((layers, groups, rows, w), jnp.float32) for w in widths]
        + [pltpu.VMEM((layers, groups - 1, rows, w), jnp.float32) for w in widths]
    )


def scatter_sems(units, groups):
    return [pltpu.SemaphoreType.DMA((units,))] * 2 + [pltpu.SemaphoreType.DMA((units, groups))] * 2


def gather_sems(units, groups):
    return [pltpu.SemaphoreType.DMA((units, groups))] * 4


def reduce_call(parts, means, squares, shard, collective):
    groups = shard // 2
    count = len(parts)
    layers, rank, _ = parts[0].shape
    rows = rank // shard
    parts = [p.reshape(layers, groups, 2, rows, p.shape[2]) for p in parts]
    widths = [p.shape[4] for p in parts]
    units = count * layers
    vmem = pl.BlockSpec(memory_space=pltpu.VMEM)
    outs = [jax.ShapeDtypeStruct(p.shape, p.dtype) for p in parts]
    outs += [jax.ShapeDtypeStruct((layers, rows, w), jnp.float32) for w in widths] * 3
    result = pl.pallas_call(
        functools.partial(reduce_kernel, groups, count),
        out_shape=outs,
        in_specs=[vmem] * (3 * count),
        out_specs=[vmem] * len(outs),
        scratch_shapes=reduce_scratch(layers, groups, rows, widths)
        + scatter_sems(units, groups)
        + gather_sems(units, groups),
        compiler_params=pltpu.CompilerParams(
            collective_id=collective, has_side_effects=True, vmem_limit_bytes=VMEM_LIMIT
        ),
        name="reduce_gather_adam",
    )(*parts, *means, *squares)
    whole = [r.reshape(layers, rank, r.shape[4]) for r in result[:count]]
    return whole, [result[count * k : count * (k + 1)] for k in range(1, 4)]


def mix(left, right):
    return jnp.dot(left, right, precision=highest, preferred_element_type=jnp.float32)


def refresh(grams):
    rank = grams[0].shape[-1]
    eye = (
        lax.broadcasted_iota(jnp.int32, (rank, rank), 0)
        == lax.broadcasted_iota(jnp.int32, (rank, rank), 1)
    ).astype(jnp.float32)
    totals = [
        jnp.sum(jnp.sum(g * eye, axis=0, keepdims=True), axis=1, keepdims=True) for g in grams
    ]
    scales = [jnp.sqrt(total) + scale_epsilon for total in totals]
    grams = [g / scale / scale for g, scale in zip(grams, scales)]
    products = None
    for sweep in range(SWEEPS):
        squared = [mix(g, g) for g in grams]
        factors = [
            coeff_linear * eye + coeff_square * g + coeff_fourth * q
            for g, q in zip(grams, squared)
        ]
        if sweep + 1 < SWEEPS:
            grams = [mix(g, f) for g, f in zip(grams, factors)]
            grams = [mix(f, g) for g, f in zip(grams, factors)]
        if products is None:
            products = factors
        else:
            products = [mix(p, f) for p, f in zip(products, factors)]
    return products, scales


def refresh_kernel(groups, count, *refs):
    def take(number):
        nonlocal refs
        head, refs = refs[:number], refs[number:]
        return head

    own, (powers,), full, (refreshed,) = take(count), take(1), take(count), take(1)
    first, half, second, sums = take(4)
    grams, gram_full = take(1), take(1)
    gram_own, pair_buf, line_buf = take(1), take(1), take(1)
    gather = Gather(groups, own, full, refs[:4], ((count - 1, 0),))
    scatter = Scatter(groups, grams, pair_buf, line_buf, gram_own, refs[4:8])
    gram_gather = Gather(groups, gram_own, gram_full, refs[8:12])
    send, recv = refs[12:]
    layers, rank = powers.shape[1], powers.shape[4]
    me = lax.axis_index("tensor")
    side, mine = lax.rem(me, 2), me // 2
    near, far = me + 1 - 2 * side, lax.rem(me + 2, 4)
    greet(groups, (near, far))
    tensor_copies = []

    def exchange(stage, src, dst, device):
        copy = remote(src, dst, send.at[stage], recv.at[stage], {"tensor": device})
        copy.start()
        tensor_copies.append(copy)
        return copy

    def arrived(stage, block, device):
        remote(block, block, send.at[stage], recv.at[stage], {"tensor": device}).wait_recv()

    far_near = exchange(0, powers.at[1 - mine, :, 1 - side], first.at[1 - mine], near)
    own_near = exchange(1, powers.at[mine, :, 1 - side], first.at[mine], near)
    units = len(gather.units)
    for u in range(units):
        gather.send(u)
    far_near.wait_recv()
    half[1 - mine] = powers[1 - mine, :, side] + first[1 - mine]
    to_far = exchange(2, half.at[1 - mine], second, far)
    own_near.wait_recv()
    half[mine] = powers[mine, :, side] + first[mine]
    for u in range(units):
        gather.turn(u)
    to_far.wait_recv()
    low, high_part = half[mine], second[...]
    sums[:, side] = low + high_part
    exchange(3, sums.at[:, side], sums.at[:, side], near)
    for u in range(units):
        if u < 2:
            gather.hop(u, 1)
    arrived(3, sums.at[:, 1 - side], near)
    for l in range(layers):
        lower, upper = sums[l, 0], sums[l, 1]
        gram = lax.dot_general(
            lower, lower, (((0,), (0,)), ((), ())), precision=highest,
            preferred_element_type=jnp.float32,
        ) + lax.dot_general(
            upper, upper, (((0,), (0,)), ((), ())), precision=highest,
            preferred_element_type=jnp.float32,
        )
        grams[0][l] = gram.reshape(grams[0].shape[1:])
        scatter.send(l)
    events = reduce_events(scatter, gram_gather, [2.0] * layers, 0.0, 3.0)
    for step in range(1, groups):
        for u in range(units):
            if step > 1 or u >= 2:
                at = (step - 2) * 18.0 + 18.0 * (u + 1) / units
                events.append((at, functools.partial(gather.hop, u, step)))
    play(events)
    for u in range(layers):
        gram_gather.landed(u)
    factors, scales = refresh([gram_full[0][l].reshape(rank, rank) for l in range(layers)])
    for l in range(layers):
        refreshed[mine, l, side] = mix(sums[l, side] / scales[l], factors[l])
    block = refreshed.at[mine, :, side]
    exchange(4, block, block, far)
    exchange(5, block, block, near)
    other = refreshed.at[1 - mine, :, side]
    arrived(4, other, far)
    exchange(6, other, other, near)
    for u in range(units):
        gather.landed(u)
    arrived(5, refreshed.at[mine, :, 1 - side], near)
    arrived(6, refreshed.at[1 - mine, :, 1 - side], near)
    for copy in tensor_copies:
        copy.wait_send()
    scatter.drain()
    gram_gather.drain()
    gather.drain()


def refresh_call(own, powers, shard, collective):
    groups = shard // 2
    count = len(own)
    layers, rows, _ = own[0].shape
    widths = [o.shape[2] for o in own]
    depth, rank = powers[0].shape[1:]
    powers = jnp.stack(powers).reshape(count, layers, 2, depth // 2, rank)
    units = count * layers
    vmem = pl.BlockSpec(memory_space=pltpu.VMEM)
    outs = [
        jax.ShapeDtypeStruct((layers, groups, 2, rows, w), jnp.float32) for w in widths
    ] + [jax.ShapeDtypeStruct(powers.shape, jnp.float32)]
    result = pl.pallas_call(
        functools.partial(refresh_kernel, groups, count),
        out_shape=outs,
        in_specs=[vmem] * (count + 1),
        out_specs=[vmem] * len(outs),
        scratch_shapes=[pltpu.VMEM((count, layers, depth // 2, rank), jnp.float32)] * 2
        + [pltpu.VMEM((layers, depth // 2, rank), jnp.float32)]
        + [pltpu.VMEM((layers, 2, depth // 2, rank), jnp.float32)]
        + [pltpu.VMEM((layers, groups, 2, rows, rank), jnp.float32)] * 2
        + reduce_scratch(layers, groups, rows, [rank])
        + gather_sems(units, groups)
        + scatter_sems(layers, groups)
        + gather_sems(layers, groups)
        + [pltpu.SemaphoreType.DMA((7,))] * 2,
        compiler_params=pltpu.CompilerParams(
            collective_id=collective, has_side_effects=True, vmem_limit_bytes=VMEM_LIMIT
        ),
        name="gather_refresh",
    )(*own, powers)
    whole = [r.reshape(layers, rank, r.shape[4]) for r in result[:count]]
    return whole, [r.reshape(layers, depth, rank) for r in result[count]]


def local(shard, *args):
    gradients, bases, moments_in = args[0:2], args[2:4], args[4:8]
    partial = [
        jnp.einsum("ldr,ldn->lrn", basis, gradient, precision=high)
        for gradient, basis in zip(gradients, bases)
    ]
    flipped = [jnp.transpose(a, (1, 0, 2)) for a in moments_in]
    projected, (moment, variance, direction) = reduce_call(
        partial, flipped[0::2], flipped[1::2], shard, 1
    )
    partial_power = [
        jnp.einsum("ldn,lrn->ldr", gradient, rows, precision=high)
        for gradient, rows in zip(gradients, projected)
    ]
    directions, refreshed = refresh_call(direction, partial_power, shard, 2)
    updates = [
        jnp.einsum("ldr,lrn->ldn", basis, rows, precision=high)
        for basis, rows in zip(bases, directions)
    ]
    back = [jnp.transpose(a, (1, 0, 2)) for pair in zip(moment, variance) for a in pair]
    return (*updates, *back, *refreshed)


def solution(mesh):
    wide, low, basis = P(None, "shard", "tensor"), P("shard", None, "tensor"), P(None, "shard", None)
    return jax.shard_map(
        functools.partial(local, mesh.shape["shard"]),
        mesh=mesh,
        in_specs=(wide, wide, basis, basis, low, low, low, low),
        out_specs=(wide, wide, low, low, low, low, basis, basis),
        check_vma=False,
    )
```
